256 devices in a mesh: section: 4 (over x), dp: 16 (over y_hi, z), tensor: 4 (over y_lo, core).
Axes of the slice: x: 4, y: 4 (y_hi: 2, y_lo: 2; y = y_hi * 2 + y_lo), z: 8, core: 2. Of those that a mesh axis runs over, the one named last changes fastest.
Arguments:
- enc_input: bfloat16 [2, 16, 128, 4096], P(None, 'dp', None, 'tensor'), may hold values from -10.8 to 10.8
- dec_input: bfloat16 [2, 16, 128, 4096], P(None, 'dp', None, 'tensor'), may hold values from -6 to 6
- lengths: int32 [2, 2, 16], P(None, None, 'dp'), may hold values from 16 to 128, as said below
- offset_bucket: int32 [2, 255], replicated, may hold values from 0 to 31
- bias_tables: float32 [2, 32, 32], P(None, None, 'tensor'), may hold values from -4.5 to 303
- norm_gain: float32 [4, 4096], P('section'), may hold values from 0.5 to 1.5
- final_gain: float32 [4096], P('tensor'), may hold values from 0.5 to 1.5
- w_query: bfloat16 [4, 4096, 2048], P('section', 'dp', 'tensor'), may hold values from -0.0234375 to 0.0234375
- w_key: bfloat16 [4, 4096, 2048], P('section', 'dp', 'tensor'), may hold values from -0.09375 to 0.09375
- w_value: bfloat16 [4, 4096, 2048], P('section', 'dp', 'tensor'), may hold values from -0.09375 to 0.09375
- w_out: bfloat16 [4, 2048, 4096], P('section', 'tensor', 'dp'), may hold values from -0.125 to 0.125
Outputs:
- section_out: bfloat16 [4, 2, 16, 128, 4096], P('section', None, 'dp', None, 'tensor')
The draws below stay inside these ranges and needn't reach their ends.
Inputs may be any that keep to these rules, and one draw needn't show every extreme that they name: In every micro-batch, sequence 0 has both lengths equal to 128.
All inputs are finite; a program needn't handle non-finite values.
Results may differ from the reference program's by a relative error of at most 0.02.
Values may be sent and summed in bfloat16 or wider, within the bound.
No kernel may reach another device: no remote copies, remote signals or barrier semaphores. Data moves between devices by JAX's collectives and lax.ppermute only.
A program may use at most 128 MiB of HBM per device.

```python
import jax
import jax.numpy as jnp
from jax import lax

D = 4096
HEADS = 32
HEAD_DIM = 64
BUCKETS = 32
MICRO = 2
L = 128
HD = 2048
SEQS = 16
N_SECTION = 4
N_TENSOR = 4


def draw_enc_input(key, part):
    shape = (MICRO, SEQS, L, D)
    column = jax.lax.broadcasted_iota(jnp.int32, shape, 3).astype(jnp.float32) / float(D - 1)
    values = jnp.clip(jax.random.normal(key, shape, jnp.float32), -6.0, 6.0)
    scale = 0.6 * jnp.exp(column * 1.0986123)
    return (values * scale).astype(jnp.bfloat16)


def draw_lengths(key, part):
    drawn = jax.random.randint(key, (MICRO, 2, SEQS), L // 8, L + 1)
    return drawn.at[:, :, 0].set(L).astype(jnp.int32)


def draw_bias_tables(key, part):
    base_key = jax.random.fold_in(key, 11)
    base_table = jax.random.normal(base_key, (2, BUCKETS, HEADS), jnp.float32) * 1.5
    return jnp.clip(base_table, -4.5, 4.5).astype(jnp.float32)


def set_ends(values, stream_key, low, top_value):
    index_at = [jax.random.randint(jax.random.fold_in(stream_key, axis), (), 0, length) for axis, length in enumerate(values.shape)]
    main_axis = values.shape.index(max(values.shape))
    next_to = index_at[:main_axis] + [(index_at[main_axis] + 1) % values.shape[main_axis]] + index_at[main_axis + 1:]
    return values.at[tuple(index_at)].set(low).at[tuple(next_to)].set(top_value)


def block_scale(key, dims, split, smallest, top_value):
    def one(position, shards_of):
        steps = jax.random.uniform(jax.random.fold_in(jax.random.fold_in(key, 6), position), (shards_of,), jnp.float32, smallest / len(split), top_value / len(split))
        return jnp.repeat(jnp.exp(steps), dims[position] // shards_of).reshape((-1,) + (1,) * (len(dims) - position - 1))

    level = one(*split[0])
    for cut in split[1:]:
        level = level * one(*cut)
    return level


def scatter_about(key, dims, scale, bound, split=(), kind=jnp.bfloat16):
    values = scale * jax.random.normal(key, dims, jnp.float32)
    if split:
        values = values * block_scale(key, dims, split, -0.22, 0.18)
    return jnp.clip(values, -bound, bound).astype(kind)


def setup_inputs(seed: int = 0) -> dict:
    arg_keys = jax.random.split(jax.random.key(seed), 12)
    return {
        "enc_input": draw_enc_input(jax.random.fold_in(arg_keys[11], 71), 0),
        "dec_input": scatter_about(arg_keys[1], (MICRO, SEQS, L, D), 1.0, 6.0, ((1, 16), (3, 4))),
        "lengths": draw_lengths(jax.random.fold_in(arg_keys[11], 71), 0),
        "offset_bucket": set_ends(jax.random.randint(arg_keys[3], (2, 2 * L - 1), 0, BUCKETS), jax.random.fold_in(arg_keys[3], 1), 0, BUCKETS - 1).astype(jnp.int32),
        "bias_tables": draw_bias_tables(jax.random.fold_in(arg_keys[11], 71), 0),
        "norm_gain": jnp.clip(1.0 + 0.1 * jax.random.normal(arg_keys[5], (N_SECTION, D), jnp.float32), 0.5, 1.5),
        "final_gain": jnp.clip(1.0 + 0.1 * jax.random.normal(arg_keys[6], (D,), jnp.float32), 0.5, 1.5),
        "w_query": scatter_about(arg_keys[7], (N_SECTION, D, HD), (D * 16) ** -0.5, 0.0234375, ((0, 4), (1, 16), (2, 4))),
        "w_key": scatter_about(arg_keys[8], (N_SECTION, D, HD), D ** -0.5, 0.09375, ((0, 4), (1, 16), (2, 4))),
        "w_value": scatter_about(arg_keys[9], (N_SECTION, D, HD), D ** -0.5, 0.09375, ((0, 4), (1, 16), (2, 4))),
        "w_out": scatter_about(arg_keys[10], (N_SECTION, HD, D), HD ** -0.5, 0.125, ((0, 4), (1, 4), (2, 16))),
    }


def scale_rows(input_rows, gain):
    single = input_rows.astype(jnp.float32)
    mean_sq = lax.optimization_barrier(jnp.mean(single * single, axis=-1, keepdims=True))
    return single * lax.rsqrt(mean_sq + 1e-06) * gain

def position_bias(bias_table, bucket_row):
    query_pos = jnp.arange(L, dtype=jnp.int32)[:, None]
    key_pos = jnp.arange(L, dtype=jnp.int32)[None, :]
    bucket = bucket_row[(key_pos - query_pos + (L - 1)).astype(jnp.int32)]
    return jnp.transpose(bias_table[bucket], (2, 0, 1)).astype(jnp.float32)

def key_mask(key_len, causal):
    query_pos = jnp.arange(L, dtype=jnp.int32)[:, None]
    key_pos = jnp.arange(L, dtype=jnp.int32)[None, :]
    allowed = key_pos[None] < key_len[:, None, None]
    if causal:
        allowed = jnp.logical_and(allowed, (key_pos <= query_pos)[None])
    return jnp.broadcast_to(allowed, (key_len.shape[0], L, L))

def project(input_rows, weight_matrix):
    return jnp.einsum('vyt,te->vye', input_rows.astype(jnp.float32), weight_matrix.astype(jnp.float32)).astype(jnp.bfloat16)

def attend(layer_normed, encoder_memory, w_query, w_key, w_value, w_out, score_bias, allowed):
    seq_count = layer_normed.shape[0]
    queries = project(layer_normed, w_query).reshape(seq_count, L, HEADS, HEAD_DIM)
    keys_proj = project(encoder_memory, w_key).reshape(seq_count, L, HEADS, HEAD_DIM)
    values = project(encoder_memory, w_value).reshape(seq_count, L, HEADS, HEAD_DIM)
    scores = jnp.einsum('sqhc,skhc->shqk', queries.astype(jnp.float32), keys_proj.astype(jnp.float32))
    scores = scores + score_bias[None]
    scores = jnp.where(allowed[:, None], scores, -1e+30)
    weights_bf = jax.nn.softmax(scores, axis=-1).astype(jnp.bfloat16)
    attended_context = jnp.einsum('shqk,skhc->sqhc', weights_bf.astype(jnp.float32), values.astype(jnp.float32)).astype(jnp.bfloat16)
    groups = attended_context.reshape(seq_count, L, N_TENSOR, HD // N_TENSOR)
    out_rows = w_out.reshape(N_TENSOR, HD // N_TENSOR, D)
    pieces = jnp.einsum('slgh,ghd->gsld', groups.astype(jnp.float32), out_rows.astype(jnp.float32)).astype(jnp.bfloat16)
    pieces = lax.optimization_barrier(pieces).astype(jnp.float32)
    return lax.optimization_barrier(jnp.sum(pieces, axis=0))

def reference(enc_input, dec_input, lengths, offset_bucket, bias_tables, norm_gain, final_gain, w_query, w_key, w_value, w_out):
    bias_enc = position_bias(bias_tables[0], offset_bucket[0])
    bias_dec = position_bias(bias_tables[1], offset_bucket[1])
    bias_none = jnp.zeros_like(bias_enc)

    def sublayer(layer_id, input_rows, encoder_memory, score_bias, allowed):
        layer_normed = scale_rows(input_rows, norm_gain[layer_id]).astype(jnp.bfloat16)
        source = layer_normed if encoder_memory is None else encoder_memory
        attended = attend(layer_normed, source, w_query[layer_id], w_key[layer_id], w_value[layer_id], w_out[layer_id], score_bias, allowed)
        return (input_rows.astype(jnp.float32) + attended).astype(jnp.bfloat16)
    by_section = [[], [], [], []]
    for micro_id in range(MICRO):
        enc_mask = key_mask(lengths[micro_id, 0], False)
        dec_mask = key_mask(lengths[micro_id, 1], True)
        encoded = sublayer(0, enc_input[micro_id], None, bias_enc, enc_mask)
        encoder_memory = scale_rows(encoded, final_gain).astype(jnp.bfloat16)
        first_out = sublayer(1, dec_input[micro_id], None, bias_dec, dec_mask)
        second = sublayer(2, first_out, encoder_memory, bias_none, enc_mask)
        third_out = sublayer(3, second, None, bias_dec, dec_mask)
        by_section[0].append(encoder_memory)
        by_section[1].append(first_out)
        by_section[2].append(second)
        by_section[3].append(third_out)
    return jnp.stack([jnp.stack(section_rows) for section_rows in by_section])
```

```python
import jax
import jax.numpy as jnp
from jax import lax
from jax.sharding import Mesh
from jax.sharding import PartitionSpec as P

D = 4096
HEAD_DIM = 64
ROWS = 256
BF = jnp.bfloat16
F32 = jnp.float32


def z_shift(value, steps):
    count = lax.axis_size("z")
    return lax.ppermute(value, "z", [(i, (i + steps) % count) for i in range(count)])


def y_swap(value, mask):
    return lax.ppermute(value, ("yhi", "ylo"), [(i, i ^ mask) for i in range(4)])


def core_swap(value):
    return lax.ppermute(value, "core", [(0, 1), (1, 0)])


def near(value):
    return y_swap(value, 1)


def far(value):
    return y_swap(value, 3)


def hop(value, source, target):
    return lax.ppermute(value, "section", [(source, target)])


def pick(pair, index):
    return jnp.where(index == 0, pair[0], pair[1])


def rms(rows, gain):
    single = rows.astype(F32)
    mean_sq = jnp.mean(single * single, axis=-1, keepdims=True)
    return (single * lax.rsqrt(mean_sq + 1e-06) * gain).astype(BF)


def spread(piece, micro):
    beside = near(piece)
    across = far(piece)
    opposite = far(beside) if micro == 0 else near(across)
    whole = []
    for first, second in ((piece, beside), (opposite, across)):
        whole.append(jnp.concatenate([first, core_swap(first), second, core_swap(second)], axis=-1))
    return jnp.stack(whole)


def collect(partial, micro):
    other = core_swap(partial[:, :, :, 1].astype(BF))
    total = partial[:, :, :, 0] + other.astype(F32)
    own, beside, opposite, across = total[0, :, 0], total[0, :, 1], total[1, :, 0], total[1, :, 1]
    if micro == 0:
        passed = near(opposite.astype(BF)).astype(F32)
        one = near(beside.astype(BF))
        two = far((across + passed).astype(BF))
    else:
        passed = far(opposite.astype(BF)).astype(F32)
        one = far(across.astype(BF))
        two = near((beside + passed).astype(BF))
    return own + one.astype(F32) + two.astype(F32)


def positional_bias(offset_bucket, bias_tables, section_id, yhi, length):
    bucket_row = jnp.where(section_id == 0, offset_bucket[0], offset_bucket[1])
    tables = jnp.where(section_id == 0, bias_tables[0], bias_tables[1])
    heads = tables.shape[1] // 2
    tables = pick((tables[:, :heads], tables[:, heads:]), yhi)
    buckets = tables.shape[0]
    row = jnp.zeros((heads, 2 * length), F32)
    padded = jnp.concatenate([bucket_row, jnp.zeros((1,), jnp.int32)])
    for bucket in range(buckets):
        row = jnp.where(padded[None] == bucket, tables[bucket][:, None], row)
    grid = jnp.broadcast_to(row[:, None, :], (heads, length, 2 * length))
    shift = length - 1 - lax.broadcasted_iota(jnp.int32, (1, length, 1), 1)
    step = 1
    while step < length:
        grid = jnp.where((shift & step) != 0, jnp.roll(grid, -step, axis=2), grid)
        step *= 2
    return grid[:, :, :length]


def attention(queries, keys, values, score_bias, allowed):
    seqs, length, width = queries.shape
    heads = width // HEAD_DIM
    q = queries.reshape(seqs, length, heads, HEAD_DIM)
    k = keys.reshape(seqs, length, heads, HEAD_DIM)
    v = values.reshape(seqs, length, heads, HEAD_DIM)
    scores = jnp.einsum("sqhc,skhc->shqk", q, k, preferred_element_type=F32)
    if score_bias is not None:
        scores = scores + score_bias[None]
    scores = jnp.where(allowed[:, None], scores, -1e30)
    highest = jnp.max(scores, axis=-1, keepdims=True)
    expsum = jnp.exp(scores - highest)
    weights = (expsum / jnp.sum(expsum, axis=-1, keepdims=True)).astype(BF)
    context = jnp.einsum("shqk,skhc->sqhc", weights, v, preferred_element_type=F32).astype(BF)
    return context.reshape(seqs, length, width)


def project(rows, weight):
    return jnp.einsum("syt,te->sye", rows, weight, preferred_element_type=F32)


def gather_ring(own, cross, place, width_axis, buffer, index):
    yhi, ylo, core, z = index
    count = lax.axis_size("z")

    def put(buffer, block, flip, source):
        z_from = lax.rem(source + count, count)
        slot = ((yhi ^ flip) ^ ylo) * 8 + ((z_from // 4) ^ core) * 4 + lax.rem(z_from, 4)
        if width_axis == 0:
            return lax.dynamic_update_slice(buffer, block[None], (slot, 0, 0))
        return lax.dynamic_update_slice(buffer, block, (0, slot * ROWS))

    buffer = put(buffer, own, 0, z)
    buffer = put(buffer, cross, 1, z)
    own_r = own_l = own
    cross_r = cross_l = cross
    half = count // 2
    for k in range(1, half + 1):
        own_r = z_shift(own_r, 1)
        buffer = put(buffer, own_r, 0, z - k)
        if k < half:
            own_l = z_shift(own_l, -1)
            buffer = put(buffer, own_l, 0, z + k)
            cross_r = z_shift(cross_r, 1)
            buffer = put(buffer, cross_r, 1, z - k)
        cross_l = z_shift(cross_l, -1)
        buffer = put(buffer, cross_l, 1, z + k)
    return buffer


def body(
    enc_input,
    dec_input,
    lengths,
    offset_bucket,
    bias_tables,
    norm_gain,
    final_gain,
    w_query,
    w_key,
    w_value,
    w_out,
):
    section_id = lax.axis_index("section")
    yhi, z = lax.axis_index("yhi"), lax.axis_index("z")
    ylo, core = lax.axis_index("ylo"), lax.axis_index("core")
    index = (yhi, ylo, core, z)
    micros, _, length, quarter = enc_input.shape
    hidden = w_query.shape[2] // 2

    halves = [
        jnp.concatenate([w[0, :, s : s + hidden] for w in (w_query, w_key, w_value)], axis=1)
        for s in (0, hidden)
    ]
    own_in = pick(halves, yhi)
    cross_in = lax.ppermute(pick(halves, 1 - yhi), "yhi", [(0, 1), (1, 0)])
    out_halves = (w_out[0, :hidden], w_out[0, hidden:])
    own_out = pick(out_halves, yhi)
    cross_out = lax.ppermute(pick(out_halves, 1 - yhi), "yhi", [(0, 1), (1, 0)])
    weight_in = gather_ring(
        own_in, cross_in, None, 0, jnp.zeros((16, ROWS, 3 * hidden), BF), index
    ).reshape(16 * ROWS, 3 * hidden)
    weight_out = gather_ring(own_out, cross_out, None, 1, jnp.zeros((hidden, D), BF), index)

    score_bias = positional_bias(offset_bucket, bias_tables, section_id, yhi, length)
    pair_lengths = jnp.concatenate(
        [lengths, lax.ppermute(lengths, "yhi", [(0, 1), (1, 0)])], axis=2
    )
    query_pos = lax.broadcasted_iota(jnp.int32, (1, length, length), 1)
    key_pos = lax.broadcasted_iota(jnp.int32, (1, length, length), 2)
    causal = key_pos <= query_pos
    gain = norm_gain[0].reshape(2, 2, quarter)
    gain = pick((gain, gain[::-1]), ylo)
    gain = pick((gain, gain[:, ::-1]), core).reshape(D)
    final_pair = jnp.concatenate([final_gain, core_swap(final_gain)])
    final_whole = jnp.concatenate([final_pair, near(final_pair)])

    def finish(piece, queries, keys, values, micro, bias, allowed):
        context = attention(queries, keys, values, bias, allowed)
        partial = project(context, weight_out).reshape(2, length, 2, 2, quarter)
        return (piece.astype(F32) + collect(partial, micro)).astype(BF)

    def self_block(piece, micro, allowed):
        rows = rms(spread(piece, micro), gain)
        mixed = project(rows, weight_in).astype(BF)
        q, k, v = (mixed[:, :, i * hidden : (i + 1) * hidden] for i in range(3))
        return finish(piece, q, k, v, micro, score_bias, allowed)

    def cross_block(piece, memory, micro, allowed):
        rows = rms(spread(piece, micro), gain)
        source = rms(spread(memory, 1 - micro), final_whole)
        q = project(rows, weight_in[:, :hidden]).astype(BF)
        kv = project(source, weight_in[:, hidden:]).astype(BF)
        return finish(piece, q, kv[:, :, :hidden], kv[:, :, hidden:], micro, None, allowed)

    firsts, seconds, thirds = [], [], []
    enc_masks, dec_masks = [], []
    for micro in range(micros):
        enc_masks.append(key_pos < pair_lengths[micro, 0][:, None, None])
        dec_masks.append(
            jnp.logical_and(key_pos < pair_lengths[micro, 1][:, None, None], causal)
        )
    for micro in range(micros):
        piece = jnp.where(section_id == 0, enc_input[micro, 0], dec_input[micro, 0])
        allowed = jnp.where(section_id == 0, enc_masks[micro], dec_masks[micro])
        firsts.append(self_block(piece, micro, allowed))
    for micro in range(micros):
        memory = hop(firsts[micro], 0, 2)
        piece = hop(firsts[micro], 1, 2)
        seconds.append(cross_block(piece, memory, micro, enc_masks[micro]))
    for micro in range(micros):
        piece = hop(seconds[micro], 2, 3)
        thirds.append(self_block(piece, micro, dec_masks[micro]))

    first = jnp.stack(firsts)
    wide = first.astype(F32)
    square = jnp.sum(wide * wide, axis=-1)
    square = square + core_swap(square)
    square = square + near(square)
    encoded = (wide * lax.rsqrt(square / D + 1e-06)[:, :, None] * final_gain).astype(BF)
    result = jnp.where(
        section_id == 0,
        encoded,
        jnp.where(
            section_id == 1,
            first,
            jnp.where(section_id == 2, jnp.stack(seconds), jnp.stack(thirds)),
        ),
    )
    return result[None, :, None]


def solution(mesh):
    sections, dp, tensor = (mesh.shape[name] for name in ("section", "dp", "tensor"))
    fine = Mesh(
        mesh.devices.reshape(sections, 2, dp // 2, tensor // 2, 2),
        ("section", "yhi", "z", "ylo", "core"),
    )
    dp, tensor = ("yhi", "z"), ("ylo", "core")
    in_specs = (
        P(None, dp, None, tensor),
        P(None, dp, None, tensor),
        P(None, None, dp),
        P(),
        P(None, None, tensor),
        P("section", None),
        P(tensor),
        P("section", dp, tensor),
        P("section", dp, tensor),
        P("section", dp, tensor),
        P("section", tensor, dp),
    )
    out_specs = P("section", None, dp, None, tensor)
    return jax.shard_map(body, mesh=fine, in_specs=in_specs, out_specs=out_specs, check_vma=False)
```

```python
import functools

import jax
import jax.numpy as jnp
from jax import lax
from jax.experimental import pallas as pl
from jax.experimental.pallas import tpu as pltpu
from jax.sharding import Mesh
from jax.sharding import PartitionSpec as P

D = 4096
HEAD_DIM = 64
ROWS = 256
BLOCKS = 16
IN_COLS = 768
L = 128
BF = jnp.bfloat16
F32 = jnp.float32


def z_shift(value, steps, sections):
    pairs = [(s * 8 + i, s * 8 + (i + steps) % 8) for s in sections for i in range(8)]
    return lax.ppermute(value, ("section", "z"), pairs)


def y_swap(value, mask, sections):
    pairs = [(s * 4 + i, s * 4 + (i ^ mask)) for s in sections for i in range(4)]
    return lax.ppermute(value, ("section", "yhi", "ylo"), pairs)


def core_swap(value, sections):
    pairs = [(s * 2 + i, s * 2 + 1 - i) for s in sections for i in range(2)]
    return lax.ppermute(value, ("section", "core"), pairs)


def hop(value, source, target):
    return lax.ppermute(value, "section", [(source, target)])


def pick(pair, index):
    return jnp.where(index == 0, pair[0], pair[1])


def arrange(first, second, gain_ref, meta, out_ref, seqs, lead):
    step = 16
    for a in range(seqs):

        def some_rows(r, carry, a=a):
            start = pl.multiple_of(r * step, step)
            chunks = []
            for f in range(4):
                source = first if f % 2 == 0 else second
                index = (a * 2 + f // 2,) if lead is None else (f // 2, lead)
                chunks.append(source[index + (pl.ds(start, step),)].astype(F32))
            square = sum(jnp.sum(c * c, axis=-1, keepdims=True) for c in chunks)
            scale = lax.rsqrt(square * (1.0 / D) + 1e-06)
            for f in range(4):
                normed = (chunks[f] * scale * gain_ref[f : f + 1, :]).astype(BF)
                for i in range(4):
                    place = pl.multiple_of(meta[f * 4 + i] * ROWS, ROWS)
                    out_ref[pl.ds(a * L + start, step), pl.ds(place, ROWS)] = normed[
                        :, i * ROWS : (i + 1) * ROWS
                    ]
            return carry

        lax.fori_loop(0, L // step, some_rows, 0)


def block_kernel(seqs, halves, cross, causal, at, on, meta, *rest):
    @pl.when(meta[on] != 0)
    def _():
        block_work(seqs, halves, cross, causal, at, meta, *rest)


def block_work(
    seqs, halves, cross, causal, at, meta, gain_ref, memory_gain, table, first, second, *rest
):
    blocks = rest[: halves * BLOCKS]
    keep, send = rest[halves * BLOCKS : halves * BLOCKS + 2]
    weights, rows, memory_rows, total, mixed, context, sems = rest[halves * BLOCKS + 2 :]
    copies = []
    for h in range(halves):
        for j in range(BLOCKS):
            copy = pltpu.make_async_copy(
                blocks[h * BLOCKS + j], weights.at[h, pl.ds(j * ROWS, ROWS), :], sems.at[h, j]
            )
            copy.start()
            copies.append(copy)
    arrange(first, second, gain_ref, meta, rows, seqs, 0 if cross else None)
    if cross:
        arrange(first, second, memory_gain, meta, memory_rows, seqs, 1)
    width = IN_COLS // 3
    pairs = width // L
    query_pos = lax.broadcasted_iota(jnp.int32, (L, L), 0)
    key_pos = lax.broadcasted_iota(jnp.int32, (L, L), 1)
    low = key_pos < HEAD_DIM
    reach = query_pos
    if causal is None:
        reach = query_pos + jnp.where(meta[32] == 0, L, 0)
    depth = 512

    for h in range(halves):
        for copy in copies[h * BLOCKS : (h + 1) * BLOCKS]:
            copy.wait()
        total[...] = jnp.zeros_like(total)

        def add_rows(k, carry, h=h):
            span = pl.ds(pl.multiple_of(k * depth, depth), depth)
            if cross:
                total[:, :width] += jnp.dot(
                    rows[:, span], weights[h, span, :width], preferred_element_type=F32
                )
                total[:, width:] += jnp.dot(
                    memory_rows[:, span],
                    weights[h, span, width:IN_COLS],
                    preferred_element_type=F32,
                )
            else:
                total[...] += jnp.dot(
                    rows[:, span], weights[h, span, :IN_COLS], preferred_element_type=F32
                )
            return carry

        lax.fori_loop(0, D // depth, add_rows, 0)
        mixed[...] = total[...].astype(BF)

        def two_heads(step, carry, h=h):
            a = step // pairs
            pair = step % pairs
            tokens = pl.ds(pl.multiple_of(a * L, L), L)
            q, k, v = (
                mixed[tokens, pl.ds(pl.multiple_of(s * width + pair * L, L), L)] for s in range(3)
            )
            nothing = jnp.zeros_like(q)
            both = jnp.concatenate([jnp.where(low, q, nothing), jnp.where(low, nothing, q)], axis=0)
            scores = lax.dot_general(both, k, (((1,), (1,)), ((), ())), preferred_element_type=F32)
            mask = key_pos < meta[at + a]
            if causal is not False:
                mask = jnp.logical_and(mask, key_pos <= reach)
            probs = []
            for n in range(2):
                part = scores[n * L : (n + 1) * L]
                if not cross:
                    line = table[pl.ds(h * 2 * pairs + pair * 2 + n, 1), :]
                    grid = pltpu.roll(
                        jnp.broadcast_to(line, (L, 2 * L)), L + 1, 1, stride=1, stride_axis=0
                    )
                    part = part + grid[:, :L]
                part = jnp.where(mask, part, -1e30)
                power = jnp.exp(part - jnp.max(part, axis=-1, keepdims=True))
                probs.append((power / jnp.sum(power, axis=-1, keepdims=True)).astype(BF))
            out = jnp.dot(jnp.concatenate(probs, axis=0), v, preferred_element_type=F32)
            context[tokens, pl.ds(pl.multiple_of(h * width + pair * L, L), L)] = jnp.where(
                low, out[:L], out[L:]
            ).astype(BF)
            return carry

        lax.fori_loop(0, seqs * pairs, two_heads, 0)

    def out_block(j, carry):
        span = pl.ds(pl.multiple_of(j * ROWS, ROWS), ROWS)
        term = None
        for h in range(halves):
            one = jnp.dot(
                context[:, h * width : (h + 1) * width],
                weights[h, span, IN_COLS:],
                preferred_element_type=F32,
            )
            term = one if term is None else term + one
        term = term.astype(BF)
        slot = meta[16 + j]
        columns = pl.ds(pl.multiple_of((slot & 3) * ROWS, ROWS), ROWS)
        for side, out in ((0, keep), (1, send)):

            @pl.when(((slot >> 2) & 1) == side)
            def _():
                for a in range(seqs):
                    out[a * 2 + (slot >> 3), :, columns] = term[a * L : (a + 1) * L]

        return carry

    lax.fori_loop(0, BLOCKS, out_block, 0)


def run_block(meta, at, on, gain, memory_gain, table, first, second, blocks, seqs, cross, causal):
    halves = len(blocks) // BLOCKS
    tokens = seqs * L
    shape = jax.ShapeDtypeStruct((2 * seqs, L, D // 4), BF)
    in_vmem = pl.BlockSpec(memory_space=pltpu.VMEM)
    flops = 2 * tokens * D * 1024 * halves
    return pl.pallas_call(
        functools.partial(block_kernel, seqs, halves, cross, causal, at, on),
        out_shape=(shape, shape),
        in_specs=[pl.BlockSpec(memory_space=pltpu.SMEM)]
        + [in_vmem] * 5
        + [pl.BlockSpec(memory_space=pl.ANY)] * len(blocks),
        out_specs=(in_vmem, in_vmem),
        scratch_shapes=[
            pltpu.VMEM((halves, BLOCKS * ROWS, 1024), BF),
            pltpu.VMEM((tokens, D), BF),
            pltpu.VMEM((tokens, D) if cross else (16, 128), BF),
            pltpu.VMEM((tokens, IN_COLS), F32),
            pltpu.VMEM((tokens, IN_COLS), BF),
            pltpu.VMEM((tokens, halves * IN_COLS // 3), BF),
            pltpu.SemaphoreType.DMA((halves, BLOCKS)),
        ],
        compiler_params=pltpu.CompilerParams(vmem_limit_bytes=48 * 1024 * 1024),
        cost_estimate=pl.CostEstimate(
            flops=flops,
            bytes_accessed=len(blocks) * ROWS * 2048 + 8 * tokens * D,
            transcendentals=0,
        ),
    )(meta, gain, memory_gain, table, first, second, *blocks)


def ring(own, right, left, sections):
    ahead, behind = [own], []
    for k in range(max(right, left)):
        if k < right:
            ahead.append(z_shift(ahead[-1], 1, sections))
        if k < left:
            last = behind[-1] if behind else own
            behind.append(z_shift(last, -1, sections))
    return ahead + behind[::-1]


def body(
    enc_input,
    dec_input,
    lengths,
    offset_bucket,
    bias_tables,
    norm_gain,
    final_gain,
    w_query,
    w_key,
    w_value,
    w_out,
):
    section_id = lax.axis_index("section")
    yhi, z = lax.axis_index("yhi"), lax.axis_index("z")
    ylo, core = lax.axis_index("ylo"), lax.axis_index("core")
    micros, _, length, quarter = enc_input.shape
    hidden = w_query.shape[2] // 2
    everywhere = (0, 1, 2, 3)

    packs = [
        jnp.concatenate(
            [w[0, :, s : s + hidden] for w in (w_query, w_key, w_value)] + [w_out[0, s : s + hidden]],
            axis=1,
        )
        for s in (0, hidden)
    ]
    own = pick(packs, yhi)
    other = pick(packs, 1 - yhi)
    own, other = lax.optimization_barrier((own, other))
    crossed = y_swap(other, 2, everywhere)
    near_list = ring(own, 4, 3, everywhere)
    cross_list = ring(crossed, 3, 4, everywhere)
    half_one = near_list + cross_list
    far_own = ring(other, 4, 3, (2, 3))
    far_cross = ring(y_swap(own, 2, (2, 3)), 3, 4, (2, 3))
    half_two = far_own + far_cross

    slots = jnp.arange(BLOCKS, dtype=jnp.int32)
    flip = (slots >> 3) ^ ylo ^ yhi
    source = (((slots >> 2) & 1) ^ core) * 4 + (slots & 3)
    place = flip * 8 + ((z - source) & 7)
    flip_of = slots >> 3
    source_of = (z - (slots & 7)) & 7
    slot_of = (flip_of ^ yhi ^ ylo) * 8 + ((source_of >> 2) ^ core) * 4 + (source_of & 3)

    across_lengths = y_swap(lengths, 2, (0, 1))
    both_lengths = jnp.concatenate([lengths, across_lengths], axis=2)
    own_lengths = jnp.where(section_id == 0, both_lengths[:, 0], both_lengths[:, 1]).reshape(4)
    flag = (section_id != 0).astype(jnp.int32)[None]
    ticks = jnp.stack([section_id < 2, section_id == 2, section_id == 3]).astype(jnp.int32)
    meta = jnp.concatenate(
        [place, slot_of, flag, own_lengths, lengths[:, 0, 0], lengths[:, 1, 0], ticks]
    )

    bucket_row = jnp.where(section_id == 0, offset_bucket[0], offset_bucket[1])
    tables = jnp.where(section_id == 0, bias_tables[0], bias_tables[1])
    tables = pick((tables, jnp.roll(tables, 4, axis=1)), yhi)
    padded = jnp.concatenate([bucket_row, jnp.zeros((1,), jnp.int32)])
    table = jnp.zeros((tables.shape[1], 2 * length), F32)
    for bucket in range(tables.shape[0]):
        table = jnp.where(padded[None] == bucket, tables[bucket][:, None], table)

    gain = norm_gain[0].reshape(2, 2, quarter)
    gain = pick((gain, gain[::-1]), ylo)
    gain = pick((gain, gain[:, ::-1]), core).reshape(4, quarter)
    final_near = y_swap(final_gain, 1, (2,))
    final_two = jnp.stack([final_gain, final_near])
    final_whole = jnp.stack([final_two, core_swap(final_two, (2,))], axis=1).reshape(4, quarter)

    def summed(keep, got, index):
        return keep[index].astype(F32) + got[index].astype(F32)

    firsts, seconds, thirds = [], [], []
    secs = (0, 1)
    for micro in range(micros):
        piece = jnp.where(section_id == 0, enc_input[micro, 0], dec_input[micro, 0])
        stack = jnp.stack([piece] + [y_swap(piece, mask, secs) for mask in (1, 2, 3)])
        swapped = core_swap(stack, secs)
        keep, send = run_block(
            meta, 33 + 2 * micro, 41, gain, gain, table, stack, swapped, half_one, 2, False, None
        )
        got = core_swap(send, secs)
        attended = summed(keep, got, 0)
        for mask in (1, 2, 3):
            back = y_swap(summed(keep, got, mask).astype(BF), mask, secs)
            attended = attended + back.astype(F32)
        firsts.append((piece.astype(F32) + attended).astype(BF))

    def combine(piece, keep, send, secs):
        got = core_swap(send, secs)
        beside = y_swap(summed(keep, got, 1).astype(BF), 1, secs)
        return (piece.astype(F32) + summed(keep, got, 0) + beside.astype(F32)).astype(BF)

    for micro in range(micros):
        piece = hop(firsts[micro], 1, 2)
        both = jnp.stack([piece, hop(firsts[micro], 0, 2)])
        stack = jnp.stack([both, y_swap(both, 1, (2,))])
        swapped = core_swap(stack, (2,))
        blocks = half_one + half_two
        keep, send = run_block(
            meta, 37 + micro, 42, gain, final_whole, table, stack, swapped, blocks, 1, True, False
        )
        seconds.append(combine(piece, keep, send, (2,)))
    for micro in range(micros):
        piece = hop(seconds[micro], 2, 3)
        stack = jnp.stack([piece, y_swap(piece, 1, (3,))])
        swapped = core_swap(stack, (3,))
        blocks = half_one + half_two
        keep, send = run_block(
            meta, 39 + micro, 43, gain, gain, table, stack, swapped, blocks, 1, False, True
        )
        thirds.append(combine(piece, keep, send, (3,)))

    first = jnp.stack(firsts)
    wide = first.astype(F32)
    square = jnp.sum(wide * wide, axis=-1)
    square = square + core_swap(square, (0,))
    square = square + y_swap(square, 1, (0,))
    encoded = (wide * lax.rsqrt(square / D + 1e-06)[:, :, None] * final_gain).astype(BF)
    early = jnp.where(section_id == 0, encoded, first)
    result = jnp.stack(
        [
            jnp.where(
                section_id == 3, thirds[m], jnp.where(section_id == 2, seconds[m], early[m])
            )
            for m in range(micros)
        ]
    )
    return result[None, :, None]


def solution(mesh):
    sections, dp, tensor = (mesh.shape[name] for name in ("section", "dp", "tensor"))
    fine = Mesh(
        mesh.devices.reshape(sections, 2, dp // 2, tensor // 2, 2),
        ("section", "yhi", "z", "ylo", "core"),
    )
    dp, tensor = ("yhi", "z"), ("ylo", "core")
    in_specs = (
        P(None, dp, None, tensor),
        P(None, dp, None, tensor),
        P(None, None, dp),
        P(),
        P(None, None, tensor),
        P("section", None),
        P(tensor),
        P("section", dp, tensor),
        P("section", dp, tensor),
        P("section", dp, tensor),
        P("section", tensor, dp),
    )
    out_specs = P("section", None, dp, None, tensor)

    return jax.shard_map(body, mesh=fine, in_specs=in_specs, out_specs=out_specs, check_vma=False)
```

```python
import functools

import jax
import jax.numpy as jnp
from jax import lax
from jax.experimental import pallas as pl
from jax.experimental.pallas import tpu as pltpu
from jax.sharding import Mesh
from jax.sharding import PartitionSpec as P

D = 4096
HEAD_DIM = 64
ROWS = 256
BLOCKS = 16
IN_COLS = 768
L = 128
BF = jnp.bfloat16
F32 = jnp.float32


def z_shift(value, steps, sections):
    pairs = [(s * 8 + i, s * 8 + (i + steps) % 8) for s in sections for i in range(8)]
    return lax.ppermute(value, ("section", "z"), pairs)


def y_swap(value, mask, sections):
    pairs = [(s * 4 + i, s * 4 + (i ^ mask)) for s in sections for i in range(4)]
    return lax.ppermute(value, ("section", "yhi", "ylo"), pairs)


def core_swap(value, sections):
    pairs = [(s * 2 + i, s * 2 + 1 - i) for s in sections for i in range(2)]
    return lax.ppermute(value, ("section", "core"), pairs)


def hop(value, source, target):
    return lax.ppermute(value, "section", [(source, target)])


def pick(pair, index):
    return jnp.where(index == 0, pair[0], pair[1])


def arrange(first, second, gain_ref, meta, out_ref, seqs, lead):
    step = 16
    for a in range(seqs):

        def some_rows(r, carry, a=a):
            start = pl.multiple_of(r * step, step)
            chunks = []
            for f in range(4):
                source = first if f % 2 == 0 else second
                index = (a * 2 + f // 2,) if lead is None else (f // 2, lead)
                chunks.append(source[index + (pl.ds(start, step),)].astype(F32))
            square = sum(jnp.sum(c * c, axis=-1, keepdims=True) for c in chunks)
            scale = lax.rsqrt(square * (1.0 / D) + 1e-06)
            for f in range(4):
                normed = (chunks[f] * scale * gain_ref[f : f + 1, :]).astype(BF)
                for i in range(4):
                    place = pl.multiple_of(meta[f * 4 + i] * ROWS, ROWS)
                    out_ref[pl.ds(a * L + start, step), pl.ds(place, ROWS)] = normed[
                        :, i * ROWS : (i + 1) * ROWS
                    ]
            return carry

        lax.fori_loop(0, L // step, some_rows, 0)


def prepare_kernel(seqs, meta, gain_ref, first, second, rows):
    @pl.when(meta[41] != 0)
    def _():
        arrange(first, second, gain_ref, meta, rows, seqs, None)


def prepare(meta, gain, first, second, seqs):
    in_vmem = pl.BlockSpec(memory_space=pltpu.VMEM)
    return pl.pallas_call(
        functools.partial(prepare_kernel, seqs),
        out_shape=jax.ShapeDtypeStruct((seqs * L, D), BF),
        in_specs=[pl.BlockSpec(memory_space=pltpu.SMEM)] + [in_vmem] * 3,
        out_specs=in_vmem,
        compiler_params=pltpu.CompilerParams(vmem_limit_bytes=16 * 1024 * 1024),
        cost_estimate=pl.CostEstimate(
            flops=8 * seqs * L * D, bytes_accessed=4 * seqs * L * D, transcendentals=0
        ),
    )(meta, gain, first, second)


def block_kernel(seqs, halves, cross, causal, ready, at, on, meta, *rest):
    @pl.when(meta[on] != 0)
    def _():
        block_work(seqs, halves, cross, causal, ready, at, meta, *rest)


def block_work(
    seqs, halves, cross, causal, ready, at, meta, gain_ref, memory_gain, table, first, second, *rest
):
    blocks = rest[: halves * BLOCKS]
    keep, send = rest[halves * BLOCKS : halves * BLOCKS + 2]
    weights, rows, memory_rows, total, mixed, context, here, partial = rest[
        halves * BLOCKS + 2 : halves * BLOCKS + 10
    ]
    sems, here_sems, exit_sems = rest[halves * BLOCKS + 10 :]
    if ready:
        entries = [pltpu.make_async_copy(first, rows, here_sems.at[0])]
    else:
        entries = [
            pltpu.make_async_copy(source, here.at[n], here_sems.at[n])
            for n, source in enumerate((first, second))
        ]
    for entry in entries:
        entry.start()
    for h in range(halves):
        for j in range(BLOCKS):
            pltpu.make_async_copy(
                blocks[h * BLOCKS + j], weights.at[h, pl.ds(j * ROWS, ROWS), :], sems.at[h, j]
            ).start()
    for entry in entries:
        entry.wait()
    first, second = here.at[0], here.at[1]
    if not ready:
        arrange(first, second, gain_ref, meta, rows, seqs, 0 if cross else None)
    if cross:
        arrange(first, second, memory_gain, meta, memory_rows, seqs, 1)
    width = IN_COLS // 3
    pairs = width // L
    query_pos = lax.broadcasted_iota(jnp.int32, (L, L), 0)
    key_pos = lax.broadcasted_iota(jnp.int32, (L, L), 1)
    low = key_pos < HEAD_DIM
    reach = query_pos
    if causal is None:
        reach = query_pos + jnp.where(meta[32] == 0, L, 0)
    depth = 1024

    for h in range(halves):
        total[...] = jnp.zeros_like(total)

        def add_rows(k, carry, h=h):
            span = pl.ds(pl.multiple_of(k * depth, depth), depth)
            for b in range(depth // ROWS):
                j = k * (depth // ROWS) + b
                landed = weights.at[h, pl.ds(pl.multiple_of(j * ROWS, ROWS), ROWS), :]
                pltpu.make_async_copy(landed, landed, sems.at[h, j]).wait()
            if cross:
                total[:, :width] += jnp.dot(
                    rows[:, span], weights[h, span, :width], preferred_element_type=F32
                )
                total[:, width:] += jnp.dot(
                    memory_rows[:, span],
                    weights[h, span, width:IN_COLS],
                    preferred_element_type=F32,
                )
            else:
                total[...] += jnp.dot(
                    rows[:, span], weights[h, span, :IN_COLS], preferred_element_type=F32
                )
            return carry

        lax.fori_loop(0, D // depth, add_rows, 0)
        mixed[...] = total[...].astype(BF)

        def two_heads(step, carry, h=h):
            a = step // pairs
            pair = step % pairs
            tokens = pl.ds(pl.multiple_of(a * L, L), L)
            q, k, v = (
                mixed[tokens, pl.ds(pl.multiple_of(s * width + pair * L, L), L)] for s in range(3)
            )
            nothing = jnp.zeros_like(q)
            both = jnp.concatenate([jnp.where(low, q, nothing), jnp.where(low, nothing, q)], axis=0)
            scores = lax.dot_general(both, k, (((1,), (1,)), ((), ())), preferred_element_type=F32)
            mask = key_pos < meta[at + a]
            if causal is not False:
                mask = jnp.logical_and(mask, key_pos <= reach)
            probs = []
            for n in range(2):
                part = scores[n * L : (n + 1) * L]
                if not cross:
                    line = table[pl.ds(h * 2 * pairs + pair * 2 + n, 1), :]
                    grid = pltpu.roll(
                        jnp.broadcast_to(line, (L, 2 * L)), L + 1, 1, stride=1, stride_axis=0
                    )
                    part = part + grid[:, :L]
                part = jnp.where(mask, part, -1e30)
                power = jnp.exp(part - jnp.max(part, axis=-1, keepdims=True))
                probs.append((power / jnp.sum(power, axis=-1, keepdims=True)).astype(BF))
            out = jnp.dot(jnp.concatenate(probs, axis=0), v, preferred_element_type=F32)
            context[tokens, pl.ds(pl.multiple_of(h * width + pair * L, L), L)] = jnp.where(
                low, out[:L], out[L:]
            ).astype(BF)
            return carry

        lax.fori_loop(0, seqs * pairs, two_heads, 0, unroll=2)

    def out_block(j, carry):
        span = pl.ds(pl.multiple_of(j * ROWS, ROWS), ROWS)
        term = None
        for h in range(halves):
            one = jnp.dot(
                context[:, h * width : (h + 1) * width],
                weights[h, span, IN_COLS:],
                preferred_element_type=F32,
            )
            term = one if term is None else term + one
        term = term.astype(BF)
        slot = meta[16 + j]
        columns = pl.ds(pl.multiple_of((slot & 3) * ROWS, ROWS), ROWS)
        for a in range(seqs):
            partial[(slot >> 2) & 1, a * 2 + (slot >> 3), :, columns] = term[a * L : (a + 1) * L]
        return carry

    lax.fori_loop(0, BLOCKS, out_block, 0, unroll=4)
    exits = [
        pltpu.make_async_copy(partial.at[side], target, exit_sems.at[side])
        for side, target in ((1, send), (0, keep))
    ]
    for leave in exits:
        leave.start()
    for leave in exits:
        leave.wait()


def run_block(meta, at, on, gain, memory_gain, table, first, second, blocks, seqs, cross, causal):
    halves = len(blocks) // BLOCKS
    tokens = seqs * L
    ready = first.ndim == 2
    shape = jax.ShapeDtypeStruct((2 * seqs, L, D // 4), BF)
    in_vmem = pl.BlockSpec(memory_space=pltpu.VMEM)
    flops = 2 * tokens * D * 1024 * halves
    return pl.pallas_call(
        functools.partial(block_kernel, seqs, halves, cross, causal, ready, at, on),
        out_shape=(shape, shape),
        in_specs=[pl.BlockSpec(memory_space=pltpu.SMEM)]
        + [in_vmem] * 3
        + [pl.BlockSpec(memory_space=pl.ANY)] * (2 + len(blocks)),
        out_specs=(pl.BlockSpec(memory_space=pl.ANY),) * 2,
        scratch_shapes=[
            pltpu.VMEM((halves, BLOCKS * ROWS, 1024), BF),
            pltpu.VMEM((tokens, D), BF),
            pltpu.VMEM((tokens, D) if cross else (16, 128), BF),
            pltpu.VMEM((tokens, IN_COLS), F32),
            pltpu.VMEM((tokens, IN_COLS), BF),
            pltpu.VMEM((tokens, halves * IN_COLS // 3), BF),
            pltpu.VMEM((2, 16, 128) if ready else (2,) + first.shape, BF),
            pltpu.VMEM((2, 2 * seqs, L, D // 4), BF),
            pltpu.SemaphoreType.DMA((halves, BLOCKS)),
            pltpu.SemaphoreType.DMA((2,)),
            pltpu.SemaphoreType.DMA((2,)),
        ],
        compiler_params=pltpu.CompilerParams(vmem_limit_bytes=48 * 1024 * 1024),
        cost_estimate=pl.CostEstimate(
            flops=flops,
            bytes_accessed=len(blocks) * ROWS * 2048 + 8 * tokens * D,
            transcendentals=0,
        ),
    )(meta, gain, memory_gain, table, first, second, *blocks)


def ring(own, right, left, sections):
    ahead, behind = [own], []
    for k in range(max(right, left)):
        if k < right:
            ahead.append(z_shift(ahead[-1], 1, sections))
        if k < left:
            last = behind[-1] if behind else own
            behind.append(z_shift(last, -1, sections))
    return ahead + behind[::-1]


def body(
    enc_input,
    dec_input,
    lengths,
    offset_bucket,
    bias_tables,
    norm_gain,
    final_gain,
    w_query,
    w_key,
    w_value,
    w_out,
):
    section_id = lax.axis_index("section")
    yhi, z = lax.axis_index("yhi"), lax.axis_index("z")
    ylo, core = lax.axis_index("ylo"), lax.axis_index("core")
    micros, _, length, quarter = enc_input.shape
    hidden = w_query.shape[2] // 2
    everywhere = (0, 1, 2, 3)

    packs = [
        jnp.concatenate(
            [w[0, :, s : s + hidden] for w in (w_query, w_key, w_value)] + [w_out[0, s : s + hidden]],
            axis=1,
        )
        for s in (0, hidden)
    ]
    own = pick(packs, yhi)
    other = pick(packs, 1 - yhi)
    own, other = lax.optimization_barrier((own, other))
    crossed = y_swap(other, 2, everywhere)
    near_list = ring(own, 4, 3, everywhere)
    cross_list = ring(crossed, 3, 4, everywhere)
    half_one = near_list + cross_list
    far_own = ring(other, 4, 3, (2, 3))
    far_cross = ring(y_swap(own, 2, (2, 3)), 3, 4, (2, 3))
    half_two = far_own + far_cross

    slots = jnp.arange(BLOCKS, dtype=jnp.int32)
    flip = (slots >> 3) ^ ylo ^ yhi
    source = (((slots >> 2) & 1) ^ core) * 4 + (slots & 3)
    place = flip * 8 + ((z - source) & 7)
    flip_of = slots >> 3
    source_of = (z - (slots & 7)) & 7
    slot_of = (flip_of ^ yhi ^ ylo) * 8 + ((source_of >> 2) ^ core) * 4 + (source_of & 3)

    across_lengths = y_swap(lengths, 2, (0, 1))
    both_lengths = jnp.concatenate([lengths, across_lengths], axis=2)
    own_lengths = jnp.where(section_id == 0, both_lengths[:, 0], both_lengths[:, 1]).reshape(4)
    flag = (section_id != 0).astype(jnp.int32)[None]
    ticks = jnp.stack([section_id < 2, section_id == 2, section_id == 3]).astype(jnp.int32)
    meta = jnp.concatenate(
        [place, slot_of, flag, own_lengths, lengths[:, 0, 0], lengths[:, 1, 0], ticks]
    )

    bucket_row = jnp.where(section_id == 0, offset_bucket[0], offset_bucket[1])
    tables = jnp.where(section_id == 0, bias_tables[0], bias_tables[1])
    tables = pick((tables, jnp.roll(tables, 4, axis=1)), yhi)
    padded = jnp.concatenate([bucket_row, jnp.zeros((1,), jnp.int32)])
    table = jnp.zeros((tables.shape[1], 2 * length), F32)
    for bucket in range(tables.shape[0]):
        table = jnp.where(padded[None] == bucket, tables[bucket][:, None], table)

    gain = norm_gain[0].reshape(2, 2, quarter)
    gain = pick((gain, gain[::-1]), ylo)
    gain = pick((gain, gain[:, ::-1]), core).reshape(4, quarter)
    final_near = y_swap(final_gain, 1, (2,))
    final_two = jnp.stack([final_gain, final_near])
    final_whole = jnp.stack([final_two, core_swap(final_two, (2,))], axis=1).reshape(4, quarter)

    def summed(keep, got, index):
        return keep[index].astype(F32) + got[index].astype(F32)

    firsts, seconds, thirds = [], [], []
    secs = (0, 1)
    for micro in range(micros):
        piece = jnp.where(section_id == 0, enc_input[micro, 0], dec_input[micro, 0])
        stack = jnp.stack([piece] + [y_swap(piece, mask, secs) for mask in (1, 2, 3)])
        swapped = core_swap(stack, secs)
        rows = prepare(meta, gain, stack, swapped, 2)
        keep, send = run_block(
            meta, 33 + 2 * micro, 41, gain, gain, table, rows, rows, half_one, 2, False, None
        )
        got = core_swap(send, secs)
        attended = summed(keep, got, 0)
        for mask in (1, 2, 3):
            back = y_swap(summed(keep, got, mask).astype(BF), mask, secs)
            attended = attended + back.astype(F32)
        firsts.append((piece.astype(F32) + attended).astype(BF))

    def combine(piece, keep, send, secs):
        got = core_swap(send, secs)
        beside = y_swap(summed(keep, got, 1).astype(BF), 1, secs)
        return (piece.astype(F32) + summed(keep, got, 0) + beside.astype(F32)).astype(BF)

    for micro in range(micros):
        piece = hop(firsts[micro], 1, 2)
        both = jnp.stack([piece, hop(firsts[micro], 0, 2)])
        stack = jnp.stack([both, y_swap(both, 1, (2,))])
        swapped = core_swap(stack, (2,))
        blocks = half_one + half_two
        keep, send = run_block(
            meta, 37 + micro, 42, gain, final_whole, table, stack, swapped, blocks, 1, True, False
        )
        seconds.append(combine(piece, keep, send, (2,)))
    for micro in range(micros):
        piece = hop(seconds[micro], 2, 3)
        stack = jnp.stack([piece, y_swap(piece, 1, (3,))])
        swapped = core_swap(stack, (3,))
        blocks = half_one + half_two
        keep, send = run_block(
            meta, 39 + micro, 43, gain, gain, table, stack, swapped, blocks, 1, False, True
        )
        thirds.append(combine(piece, keep, send, (3,)))

    first = jnp.stack(firsts)
    wide = first.astype(F32)
    square = jnp.sum(wide * wide, axis=-1)
    square = square + core_swap(square, (0,))
    square = square + y_swap(square, 1, (0,))
    encoded = (wide * lax.rsqrt(square / D + 1e-06)[:, :, None] * final_gain).astype(BF)
    early = jnp.where(section_id == 0, encoded, first)
    result = jnp.stack(
        [
            jnp.where(
                section_id == 3, thirds[m], jnp.where(section_id == 2, seconds[m], early[m])
            )
            for m in range(micros)
        ]
    )
    return result[None, :, None]


def solution(mesh):
    sections, dp, tensor = (mesh.shape[name] for name in ("section", "dp", "tensor"))
    fine = Mesh(
        mesh.devices.reshape(sections, 2, dp // 2, tensor // 2, 2),
        ("section", "yhi", "z", "ylo", "core"),
    )
    dp, tensor = ("yhi", "z"), ("ylo", "core")
    in_specs = (
        P(None, dp, None, tensor),
        P(None, dp, None, tensor),
        P(None, None, dp),
        P(),
        P(None, None, tensor),
        P("section", None),
        P(tensor),
        P("section", dp, tensor),
        P("section", dp, tensor),
        P("section", dp, tensor),
        P("section", tensor, dp),
    )
    out_specs = P("section", None, dp, None, tensor)

    return jax.shard_map(body, mesh=fine, in_specs=in_specs, out_specs=out_specs, check_vma=False)
```

```python
import functools

import jax
import jax.numpy as jnp
from jax import lax
from jax.experimental import pallas as pl
from jax.experimental.pallas import tpu as pltpu
from jax.sharding import Mesh
from jax.sharding import PartitionSpec as P

D = 4096
HEAD_DIM = 64
ROWS = 256
BLOCKS = 16
IN_COLS = 768
L = 128
BF = jnp.bfloat16
F32 = jnp.float32


def z_shift(value, steps, sections):
    pairs = [(s * 8 + i, s * 8 + (i + steps) % 8) for s in sections for i in range(8)]
    return lax.ppermute(value, ("section", "z"), pairs)


def y_swap(value, mask, sections):
    pairs = [(s * 4 + i, s * 4 + (i ^ mask)) for s in sections for i in range(4)]
    return lax.ppermute(value, ("section", "yhi", "ylo"), pairs)


def core_swap(value, sections):
    pairs = [(s * 2 + i, s * 2 + 1 - i) for s in sections for i in range(2)]
    return lax.ppermute(value, ("section", "core"), pairs)


def hop(value, source, target):
    return lax.ppermute(value, "section", [(source, target)])


def pick(pair, index):
    return jnp.where(index == 0, pair[0], pair[1])


def arrange(first, second, gain_ref, meta, out_ref, seqs, lead):
    step = 16
    for a in range(seqs):

        def some_rows(r, carry, a=a):
            start = pl.multiple_of(r * step, step)
            chunks = []
            for f in range(4):
                source = first if f % 2 == 0 else second
                index = (a * 2 + f // 2,) if lead is None else (f // 2, lead)
                chunks.append(source[index + (pl.ds(start, step),)].astype(F32))
            square = sum(jnp.sum(c * c, axis=-1, keepdims=True) for c in chunks)
            scale = lax.rsqrt(square * (1.0 / D) + 1e-06)
            for f in range(4):
                normed = (chunks[f] * scale * gain_ref[f : f + 1, :]).astype(BF)
                for i in range(4):
                    place = pl.multiple_of(meta[f * 4 + i] * ROWS, ROWS)
                    out_ref[pl.ds(a * L + start, step), pl.ds(place, ROWS)] = normed[
                        :, i * ROWS : (i + 1) * ROWS
                    ]
            return carry

        lax.fori_loop(0, L // step, some_rows, 0)


def prepare_kernel(seqs, meta, gain_ref, first, second, rows):
    @pl.when(meta[41] != 0)
    def _():
        arrange(first, second, gain_ref, meta, rows, seqs, None)


def prepare(meta, gain, first, second, seqs):
    in_vmem = pl.BlockSpec(memory_space=pltpu.VMEM)
    return pl.pallas_call(
        functools.partial(prepare_kernel, seqs),
        out_shape=jax.ShapeDtypeStruct((seqs * L, D), BF),
        in_specs=[pl.BlockSpec(memory_space=pltpu.SMEM)] + [in_vmem] * 3,
        out_specs=in_vmem,
        compiler_params=pltpu.CompilerParams(vmem_limit_bytes=16 * 1024 * 1024),
        cost_estimate=pl.CostEstimate(
            flops=8 * seqs * L * D, bytes_accessed=4 * seqs * L * D, transcendentals=0
        ),
    )(meta, gain, first, second)


def block_kernel(seqs, halves, cross, causal, ready, at, on, meta, *rest):
    @pl.when(meta[on] != 0)
    def _():
        block_work(seqs, halves, cross, causal, ready, at, meta, *rest)


def block_work(
    seqs, halves, cross, causal, ready, at, meta, gain_ref, memory_gain, table, first, second, *rest
):
    blocks = rest[: halves * BLOCKS]
    keep, send = rest[halves * BLOCKS : halves * BLOCKS + 2]
    weights, rows, memory_rows, total, mixed, context, here, partial = rest[
        halves * BLOCKS + 2 : halves * BLOCKS + 10
    ]
    sems, here_sems, exit_sems = rest[halves * BLOCKS + 10 :]
    if ready:
        entries = [pltpu.make_async_copy(first, rows, here_sems.at[0])]
    else:
        entries = [
            pltpu.make_async_copy(source, here.at[n], here_sems.at[n])
            for n, source in enumerate((first, second))
        ]
    for entry in entries:
        entry.start()
    for h in range(halves):
        for j in range(BLOCKS):
            pltpu.make_async_copy(
                blocks[h * BLOCKS + j], weights.at[h, pl.ds(j * ROWS, ROWS), :], sems.at[h, j]
            ).start()
    for entry in entries:
        entry.wait()
    first, second = here.at[0], here.at[1]
    if not ready:
        arrange(first, second, gain_ref, meta, rows, seqs, 0 if cross else None)
    if cross:
        arrange(first, second, memory_gain, meta, memory_rows, seqs, 1)
    width = IN_COLS // 3
    pairs = width // L
    query_pos = lax.broadcasted_iota(jnp.int32, (L, L), 0)
    key_pos = lax.broadcasted_iota(jnp.int32, (L, L), 1)
    low = key_pos < HEAD_DIM
    reach = query_pos
    if causal is None:
        reach = query_pos + jnp.where(meta[32] == 0, L, 0)
    depth = 1024

    for h in range(halves):
        total[...] = jnp.zeros_like(total)

        def add_rows(k, carry, h=h):
            span = pl.ds(pl.multiple_of(k * depth, depth), depth)
            for b in range(depth // ROWS):
                j = k * (depth // ROWS) + b
                landed = weights.at[h, pl.ds(pl.multiple_of(j * ROWS, ROWS), ROWS), :]
                pltpu.make_async_copy(landed, landed, sems.at[h, j]).wait()
            if cross:
                total[:, :width] += jnp.dot(
                    rows[:, span], weights[h, span, :width], preferred_element_type=F32
                )
                total[:, width:] += jnp.dot(
                    memory_rows[:, span],
                    weights[h, span, width:IN_COLS],
                    preferred_element_type=F32,
                )
            else:
                total[...] += jnp.dot(
                    rows[:, span], weights[h, span, :IN_COLS], preferred_element_type=F32
                )
            return carry

        lax.fori_loop(0, D // depth, add_rows, 0)
        mixed[...] = total[...].astype(BF)

        def two_heads(step, carry, h=h):
            a = step // pairs
            pair = step % pairs
            tokens = pl.ds(pl.multiple_of(a * L, L), L)
            q, k, v = (
                mixed[tokens, pl.ds(pl.multiple_of(s * width + pair * L, L), L)] for s in range(3)
            )
            nothing = jnp.zeros_like(q)
            both = jnp.concatenate([jnp.where(low, q, nothing), jnp.where(low, nothing, q)], axis=0)
            scores = lax.dot_general(both, k, (((1,), (1,)), ((), ())), preferred_element_type=F32)
            mask = key_pos < meta[at + a]
            if causal is not False:
                mask = jnp.logical_and(mask, key_pos <= reach)
            probs = []
            for n in range(2):
                part = scores[n * L : (n + 1) * L]
                if not cross:
                    line = table[pl.ds(h * 2 * pairs + pair * 2 + n, 1), :]
                    grid = pltpu.roll(
                        jnp.broadcast_to(line, (L, 2 * L)), L + 1, 1, stride=1, stride_axis=0
                    )
                    part = part + grid[:, :L]
                part = jnp.where(mask, part, -1e30)
                power = jnp.exp(part - jnp.max(part, axis=-1, keepdims=True))
                probs.append((power / jnp.sum(power, axis=-1, keepdims=True)).astype(BF))
            out = jnp.dot(jnp.concatenate(probs, axis=0), v, preferred_element_type=F32)
            context[tokens, pl.ds(pl.multiple_of(h * width + pair * L, L), L)] = jnp.where(
                low, out[:L], out[L:]
            ).astype(BF)
            return carry

        lax.fori_loop(0, seqs * pairs, two_heads, 0, unroll=2)

    def out_block(j, carry):
        span = pl.ds(pl.multiple_of(j * ROWS, ROWS), ROWS)
        term = None
        for h in range(halves):
            one = jnp.dot(
                context[:, h * width : (h + 1) * width],
                weights[h, span, IN_COLS:],
                preferred_element_type=F32,
            )
            term = one if term is None else term + one
        term = term.astype(BF)
        slot = meta[16 + j]
        columns = pl.ds(pl.multiple_of((slot & 3) * ROWS, ROWS), ROWS)
        for a in range(seqs):
            partial[(slot >> 2) & 1, a * 2 + (slot >> 3), :, columns] = term[a * L : (a + 1) * L]
        return carry

    lax.fori_loop(0, BLOCKS, out_block, 0, unroll=4)
    exits = [
        pltpu.make_async_copy(partial.at[side], target, exit_sems.at[side])
        for side, target in ((1, send), (0, keep))
    ]
    for leave in exits:
        leave.start()
    for leave in exits:
        leave.wait()


def run_block(meta, at, on, gain, memory_gain, table, first, second, blocks, seqs, cross, causal):
    halves = len(blocks) // BLOCKS
    tokens = seqs * L
    ready = first.ndim == 2
    shape = jax.ShapeDtypeStruct((2 * seqs, L, D // 4), BF)
    in_vmem = pl.BlockSpec(memory_space=pltpu.VMEM)
    flops = 2 * tokens * D * 1024 * halves
    return pl.pallas_call(
        functools.partial(block_kernel, seqs, halves, cross, causal, ready, at, on),
        out_shape=(shape, shape),
        in_specs=[pl.BlockSpec(memory_space=pltpu.SMEM)]
        + [in_vmem] * 3
        + [pl.BlockSpec(memory_space=pl.ANY)] * (2 + len(blocks)),
        out_specs=(pl.BlockSpec(memory_space=pl.ANY),) * 2,
        scratch_shapes=[
            pltpu.VMEM((halves, BLOCKS * ROWS, 1024), BF),
            pltpu.VMEM((tokens, D), BF),
            pltpu.VMEM((tokens, D) if cross else (16, 128), BF),
            pltpu.VMEM((tokens, IN_COLS), F32),
            pltpu.VMEM((tokens, IN_COLS), BF),
            pltpu.VMEM((tokens, halves * IN_COLS // 3), BF),
            pltpu.VMEM((2, 16, 128) if ready else (2,) + first.shape, BF),
            pltpu.VMEM((2, 2 * seqs, L, D // 4), BF),
            pltpu.SemaphoreType.DMA((halves, BLOCKS)),
            pltpu.SemaphoreType.DMA((2,)),
            pltpu.SemaphoreType.DMA((2,)),
        ],
        compiler_params=pltpu.CompilerParams(vmem_limit_bytes=48 * 1024 * 1024),
        cost_estimate=pl.CostEstimate(
            flops=flops,
            bytes_accessed=len(blocks) * ROWS * 2048 + 8 * tokens * D,
            transcendentals=0,
        ),
    )(meta, gain, memory_gain, table, first, second, *blocks)


def ring(own, right, left, sections):
    ahead, behind = [own], []
    for k in range(max(right, left)):
        if k < right:
            ahead.append(z_shift(ahead[-1], 1, sections))
        if k < left:
            last = behind[-1] if behind else own
            behind.append(z_shift(last, -1, sections))
    return ahead + behind[::-1]


def body(
    enc_input,
    dec_input,
    lengths,
    offset_bucket,
    bias_tables,
    norm_gain,
    final_gain,
    w_query,
    w_key,
    w_value,
    w_out,
):
    section_id = lax.axis_index("section")
    yhi, z = lax.axis_index("yhi"), lax.axis_index("z")
    ylo, core = lax.axis_index("ylo"), lax.axis_index("core")
    micros, _, length, quarter = enc_input.shape
    hidden = w_query.shape[2] // 2
    everywhere = (0, 1, 2, 3)

    packs = [
        jnp.concatenate(
            [w[0, :, s : s + hidden] for w in (w_query, w_key, w_value)] + [w_out[0, s : s + hidden]],
            axis=1,
        )
        for s in (0, hidden)
    ]
    own = pick(packs, yhi)
    other = pick(packs, 1 - yhi)
    own, other = lax.optimization_barrier((own, other))
    crossed = y_swap(other, 2, everywhere)
    near_list = ring(own, 4, 3, everywhere)
    cross_list = ring(crossed, 3, 4, everywhere)
    half_one = near_list + cross_list
    far_own = ring(other, 5, 2, (2, 3))
    far_left = ring(y_swap(own, 2, (2, 3)), 0, 4, (2, 3))
    far_near = [y_swap(near_list[k], 2, (2, 3)) for k in (1, 2, 3)]
    far_cross = far_left[:1] + far_near + far_left[1:]
    half_two = far_own + far_cross

    slots = jnp.arange(BLOCKS, dtype=jnp.int32)
    flip = (slots >> 3) ^ ylo ^ yhi
    source = (((slots >> 2) & 1) ^ core) * 4 + (slots & 3)
    place = flip * 8 + ((z - source) & 7)
    flip_of = slots >> 3
    source_of = (z - (slots & 7)) & 7
    slot_of = (flip_of ^ yhi ^ ylo) * 8 + ((source_of >> 2) ^ core) * 4 + (source_of & 3)

    across_lengths = y_swap(lengths, 2, (0, 1))
    both_lengths = jnp.concatenate([lengths, across_lengths], axis=2)
    own_lengths = jnp.where(section_id == 0, both_lengths[:, 0], both_lengths[:, 1]).reshape(4)
    flag = (section_id != 0).astype(jnp.int32)[None]
    ticks = jnp.stack([section_id < 2, section_id == 2, section_id == 3]).astype(jnp.int32)
    meta = jnp.concatenate(
        [place, slot_of, flag, own_lengths, lengths[:, 0, 0], lengths[:, 1, 0], ticks]
    )

    bucket_row = jnp.where(section_id == 0, offset_bucket[0], offset_bucket[1])
    tables = jnp.where(section_id == 0, bias_tables[0], bias_tables[1])
    tables = pick((tables, jnp.roll(tables, 4, axis=1)), yhi)
    padded = jnp.concatenate([bucket_row, jnp.zeros((1,), jnp.int32)])
    table = jnp.zeros((tables.shape[1], 2 * length), F32)
    for bucket in range(tables.shape[0]):
        table = jnp.where(padded[None] == bucket, tables[bucket][:, None], table)

    gain = norm_gain[0].reshape(2, 2, quarter)
    gain = pick((gain, gain[::-1]), ylo)
    gain = pick((gain, gain[:, ::-1]), core).reshape(4, quarter)
    final_near = y_swap(final_gain, 1, (2,))
    final_two = jnp.stack([final_gain, final_near])
    final_whole = jnp.stack([final_two, core_swap(final_two, (2,))], axis=1).reshape(4, quarter)

    def summed(keep, got, index):
        return keep[index].astype(F32) + got[index].astype(F32)

    firsts, seconds, thirds = [], [], []
    secs = (0, 1)
    for micro in range(micros):
        piece = jnp.where(section_id == 0, enc_input[micro, 0], dec_input[micro, 0])
        stack = jnp.stack([piece] + [y_swap(piece, mask, secs) for mask in (1, 2, 3)])
        swapped = core_swap(stack, secs)
        rows = prepare(meta, gain, stack, swapped, 2)
        keep, send = run_block(
            meta, 33 + 2 * micro, 41, gain, gain, table, rows, rows, half_one, 2, False, None
        )
        got = core_swap(send, secs)
        attended = summed(keep, got, 0)
        for mask in (1, 2, 3):
            back = y_swap(summed(keep, got, mask).astype(BF), mask, secs)
            attended = attended + back.astype(F32)
        firsts.append((piece.astype(F32) + attended).astype(BF))

    def combine(piece, keep, send, secs):
        got = core_swap(send, secs)
        beside = y_swap(summed(keep, got, 1).astype(BF), 1, secs)
        return (piece.astype(F32) + summed(keep, got, 0) + beside.astype(F32)).astype(BF)

    for micro in range(micros):
        piece = hop(firsts[micro], 1, 2)
        both = jnp.stack([piece, hop(firsts[micro], 0, 2)])
        stack = jnp.stack([both, y_swap(both, 1, (2,))])
        swapped = core_swap(stack, (2,))
        blocks = half_one + half_two
        keep, send = run_block(
            meta, 37 + micro, 42, gain, final_whole, table, stack, swapped, blocks, 1, True, False
        )
        seconds.append(combine(piece, keep, send, (2,)))
    for micro in range(micros):
        piece = hop(seconds[micro], 2, 3)
        stack = jnp.stack([piece, y_swap(piece, 1, (3,))])
        swapped = core_swap(stack, (3,))
        blocks = half_one + half_two
        keep, send = run_block(
            meta, 39 + micro, 43, gain, gain, table, stack, swapped, blocks, 1, False, True
        )
        thirds.append(combine(piece, keep, send, (3,)))

    first = jnp.stack(firsts)
    wide = first.astype(F32)
    square = jnp.sum(wide * wide, axis=-1)
    square = square + core_swap(square, (0,))
    square = square + y_swap(square, 1, (0,))
    encoded = (wide * lax.rsqrt(square / D + 1e-06)[:, :, None] * final_gain).astype(BF)
    early = jnp.where(section_id == 0, encoded, first)
    result = jnp.stack(
        [
            jnp.where(
                section_id == 3, thirds[m], jnp.where(section_id == 2, seconds[m], early[m])
            )
            for m in range(micros)
        ]
    )
    return result[None, :, None]


def solution(mesh):
    sections, dp, tensor = (mesh.shape[name] for name in ("section", "dp", "tensor"))
    fine = Mesh(
        mesh.devices.reshape(sections, 2, dp // 2, tensor // 2, 2),
        ("section", "yhi", "z", "ylo", "core"),
    )
    dp, tensor = ("yhi", "z"), ("ylo", "core")
    in_specs = (
        P(None, dp, None, tensor),
        P(None, dp, None, tensor),
        P(None, None, dp),
        P(),
        P(None, None, tensor),
        P("section", None),
        P(tensor),
        P("section", dp, tensor),
        P("section", dp, tensor),
        P("section", dp, tensor),
        P("section", tensor, dp),
    )
    out_specs = P("section", None, dp, None, tensor)

    return jax.shard_map(body, mesh=fine, in_specs=in_specs, out_specs=out_specs, check_vma=False)
```
